32 devices in a mesh: dp: 2 (over y), head: 4 (over z), mlp: 4 (over x, core).
Axes of the slice: x: 2, y: 2, z: 4, core: 2. Of those that a mesh axis runs over, the one named last changes fastest.
Arguments:
- block_input: float32 [12288, 1024], P(('dp', 'head', 'mlp')), may hold values from -6 to 6
- first_values: bfloat16 [12288, 1024], P('dp', ('head', 'mlp')), may hold values from -6 to 6
- lengths: int32 [2, 4], P('dp'), may hold values from 1 to 3072, 6144 in all within a row
- key_mask: int32 [12288], P('dp'), may hold values 0 or 1
- attn_gain: float32 [1024], replicated, may hold values from 0.5 to 1.5
- query_weight: bfloat16 [1024, 1024], P(None, ('head', 'mlp')), may hold values from -0.1875 to 0.1875
- key_weight: bfloat16 [1024, 1024], P(None, ('head', 'mlp')), may hold values from -0.1875 to 0.1875
- value_weight: bfloat16 [1024, 1024], P(None, ('head', 'mlp')), may hold values from -0.1875 to 0.1875
- out_weight: bfloat16 [1024, 1024], P(('head', 'mlp')), may hold values from -3 to 3
- mixer_gain: float32 [1024], replicated, may hold values from 0.5 to 1.5
- gate_weight: bfloat16 [1024, 2816], P(None, 'mlp'), may hold values from -0.1875 to 0.1875
- up_weight: bfloat16 [1024, 2816], P(None, 'mlp'), may hold values from -0.1875 to 0.1875
- down_weight: bfloat16 [2816, 1024], P('mlp'), may hold values from -0.15625 to 0.15625
- cotangent: float32 [12288, 1024], P(('dp', 'head', 'mlp')), may hold values from -6 to 6
Outputs:
- block_output: float32 [12288, 1024], P(('dp', 'head', 'mlp'))
- input_grad: float32 [12288, 1024], P(('dp', 'head', 'mlp'))
- first_values_grad: float32 [12288, 1024], P('dp', ('head', 'mlp'))
- query_grad: float32 [1024, 1024], P(None, ('head', 'mlp'))
- key_grad: float32 [1024, 1024], P(None, ('head', 'mlp'))
- value_grad: float32 [1024, 1024], P(None, ('head', 'mlp'))
- out_grad: float32 [1024, 1024], P(('head', 'mlp'))
- attn_gain_grad: float32 [1024], replicated
- mixer_gain_grad: float32 [1024], replicated
- gate_grad: float32 [1024, 2816], P(None, 'mlp')
- up_grad: float32 [1024, 2816], P(None, 'mlp')
- down_grad: float32 [2816, 1024], P('mlp')
The draws below stay inside these ranges and needn't reach their ends.
Inputs may be any that keep to these rules, and one draw needn't show every extreme that they name: Each row of lengths sums to 6144, and its largest entry is exactly 3072.
All inputs are finite; a program needn't handle non-finite values. No bound on the sum of `key_mask` on one device may be relied on, other than what follows from the above.
Results may differ from the reference program's by a relative error of at most 0.019.
Values may be sent and summed in bfloat16 or wider, within the bound.
No kernel may reach another device: no remote copies, remote signals or barrier semaphores. Data moves between devices by JAX's collectives and lax.ppermute only.
A program may use at most 192 MiB of HBM per device.

```python
import math
import jax
import jax.numpy as jnp
import numpy as np
from jax import lax

D = 1024
HEADS = 16
HD = 64
FF = 2816
SEQS = 4
GROUP = 6144
MOST = 3072
TOKENS = 12288
N_DP = 2


def place_ends(entries, key, least, high):
    index_at = [jax.random.randint(jax.random.fold_in(key, axis), (), 0, length) for axis, length in enumerate(entries.shape)]
    widest = entries.shape.index(max(entries.shape))
    neighbour = index_at[:widest] + [(index_at[widest] + 1) % entries.shape[widest]] + index_at[widest + 1:]
    return entries.at[tuple(index_at)].set(least).at[tuple(neighbour)].set(high)


def level_of(stream_key, shape, cuts, smallest, largest):
    def one(axis_at, parts):
        draws = jax.random.uniform(jax.random.fold_in(jax.random.fold_in(stream_key, 6), axis_at), (parts,), jnp.float32, smallest / len(cuts), largest / len(cuts))
        return jnp.repeat(jnp.exp(draws), shape[axis_at] // parts).reshape((-1,) + (1,) * (len(shape) - axis_at - 1))

    level = one(*cuts[0])
    for cut in cuts[1:]:
        level = level * one(*cut)
    return level


def profile(number_of, total, bound, lean):
    loads = [(1 << 20) // math.isqrt(grade ** lean) + 1 for grade in range(2, number_of + 1)]
    spare, given = total - bound - (number_of - 1), [1] * (number_of - 1)
    while spare > 0:
        movable = [i for i in range(number_of - 1) if given[i] < bound]
        pool, remaining = sum([loads[i] for i in movable]), spare
        for i in movable:
            addition = min(bound - given[i], max(1, remaining * loads[i] // pool), spare)
            given[i] = given[i] + addition
            spare = spare - addition
    return np.array([bound] + given)


def ragged_sizes(rng, count, total, most, skew):
    if count == 2:
        one = jax.random.randint(rng, (), max(1, total - most), min(most, total - 1) + 1)
        return jnp.stack([one, total - one])
    tallies = jnp.asarray(profile(count, total, most, skew), jnp.int32)
    pairs = (count - 1) // 2
    giver, taker = tallies[1:1 + 2 * pairs:2], tallies[2:2 + 2 * pairs:2]
    room = jnp.minimum(giver - 1, most - taker)
    passed = jax.random.randint(jax.random.fold_in(rng, 1), (pairs,), 0, 1 << 20) % (room + 1)
    tallies = tallies.at[1:1 + 2 * pairs:2].set(giver - passed).at[2:2 + 2 * pairs:2].set(taker + passed)
    return tallies[jax.random.permutation(jax.random.fold_in(rng, 2), count)]


def bell_draw(key, dims, deviation, limit, shards=(), kind=jnp.bfloat16):
    level = level_of(key, dims, shards, -0.22, 0.18) if shards else 1.0
    array = jax.random.normal(key, dims, jnp.float32) * deviation * level
    return jnp.minimum(jnp.maximum(array, -limit), limit).astype(kind)


def setup_inputs(seed: int = 0) -> dict:
    seeds = jax.random.split(jax.random.key(seed), 15)
    return {
        "block_input": bell_draw(seeds[0], (TOKENS, D), 1.0, 6.0, ((0, 32),), jnp.float32),
        "first_values": bell_draw(seeds[1], (TOKENS, HEADS * HD), 1.0, 6.0, ((0, 2), (1, 16))),
        "lengths": jax.vmap(lambda own: ragged_sizes(own, SEQS, GROUP, MOST, 2))(jax.random.split(seeds[2], N_DP)).reshape((N_DP, SEQS)).astype(jnp.int32),
        "key_mask": place_ends((jax.random.randint(seeds[3], (TOKENS,), 0, 8) < 7).astype(jnp.int32), jax.random.fold_in(seeds[3], 1), 0, 1),
        "attn_gain": jnp.clip(1.0 + 0.1 * jax.random.normal(seeds[4], (D,), jnp.float32), 0.5, 1.5),
        "query_weight": bell_draw(seeds[5], (D, HEADS * HD), D ** -0.5, 0.1875, ((1, 16),)),
        "key_weight": bell_draw(seeds[6], (D, HEADS * HD), D ** -0.5, 0.1875, ((1, 16),)),
        "value_weight": bell_draw(seeds[7], (D, HEADS * HD), D ** -0.5, 0.1875, ((1, 16),)),
        "out_weight": bell_draw(seeds[8], (HEADS * HD, D), (max(HD // 16, 1)) ** -0.5, 3.0, ((0, 16),)),
        "mixer_gain": jnp.clip(1.0 + 0.1 * jax.random.normal(seeds[9], (D,), jnp.float32), 0.5, 1.5),
        "gate_weight": bell_draw(seeds[10], (D, FF), D ** -0.5, 0.1875, ((1, 4),)),
        "up_weight": bell_draw(seeds[11], (D, FF), D ** -0.5, 0.1875, ((1, 4),)),
        "down_weight": bell_draw(seeds[12], (FF, D), (FF // 2) ** -0.5, 0.15625, ((0, 4),)),
        "cotangent": bell_draw(seeds[13], (TOKENS, D), 1.0, 6.0, ((0, 32),), jnp.float32),
    }


@jax.custom_vjp
def low(v):
    return lax.optimization_barrier(v.astype(jnp.bfloat16)).astype(jnp.float32)

@jax.custom_vjp
def low_back(v):
    return v

def low_keep(v):
    return (low(v), None)

def low_pass(kept, grad):
    return (grad,)

def back_keep(v):
    return (v, None)

def back_low(kept, grad):
    return (low(grad),)
low.defvjp(low_keep, low_pass)
low_back.defvjp(back_keep, back_low)
epsilon = 1e-05
masked_score = -1e+30
mix_weight = 0.5
highest = lax.Precision.HIGHEST

def matmul(left, right):
    return jnp.dot(left, right, precision=highest)

def layout(lengths, group_rows):
    ends = jnp.cumsum(lengths, axis=-1)
    starts = ends - lengths
    index = jnp.arange(group_rows, dtype=jnp.int32)
    segment = lax.optimization_barrier(jnp.sum((index[None, :, None] >= ends[:, None, :-1]).astype(jnp.int32), axis=-1))
    number = jnp.arange(lengths.shape[-1], dtype=jnp.int32)
    start_of = lax.optimization_barrier(jnp.sum(jnp.where(segment[..., None] == number, starts[:, None, :], 0), axis=-1))
    return (segment, index[None, :] - start_of)

def rope_tables(position):
    half_dim = HD // 2
    freqs = 10000.0 ** (-2.0 * jnp.arange(half_dim, dtype=jnp.float32) / HD)
    angles = position.astype(jnp.float32)[..., None] * freqs
    return (jnp.cos(angles), jnp.sin(angles))

def rotate(values, cosine, sine):
    half_dim = values.shape[-1] // 2
    first, second = (values[..., :half_dim], values[..., half_dim:])
    cos_b = cosine[:, None, :]
    sin_b = sine[:, None, :]
    return jnp.concatenate([first * cos_b - second * sin_b, second * cos_b + first * sin_b], axis=-1)

def rms(values, gain):
    return values * lax.rsqrt(lax.optimization_barrier(jnp.mean(values * values, axis=-1, keepdims=True)) + epsilon) * gain

def attend_block(query_block, key_rows, value_rows, query_index, query_segment, key_segment, key_mask):
    key_index = jnp.arange(key_rows.shape[0], dtype=jnp.int32)
    raw_scores = low_back(jnp.einsum('bhd,khd->hbk', query_block, key_rows, precision=highest))
    scores = raw_scores * HD ** (-0.5)
    allowed = (query_segment[:, None] == key_segment[None, :]) & (key_index[None, :] <= query_index[:, None]) & ((key_mask[None, :] == 1) | (key_index[None, :] == query_index[:, None]))
    scores = jnp.where(allowed[None], scores, masked_score)
    log_total = jax.nn.logsumexp(scores, axis=-1, keepdims=True)
    attn_weights = low(jnp.exp(scores - log_total))
    return jnp.einsum('hbk,khd->bhd', attn_weights, value_rows, precision=highest)

def attend_group(packed):
    query_group, key_rows, value_rows, segment, key_mask = packed
    block_rows = min(512, GROUP)
    block_count = GROUP // block_rows
    head_count = query_group.shape[1]
    index = jnp.arange(GROUP, dtype=jnp.int32)
    step_fn = jax.checkpoint(attend_block)

    def one_block(blocked_item):
        return step_fn(blocked_item[0], key_rows, value_rows, blocked_item[1], blocked_item[2], segment, key_mask)
    blocked = (query_group.reshape(block_count, block_rows, head_count, HD), index.reshape(block_count, block_rows), segment.reshape(block_count, block_rows))
    result = lax.map(one_block, blocked)
    return result.reshape(GROUP, head_count, HD)

def forward(x_rows, first_rows, gain_one, query_weight, key_weight, value_weight, out_weight, gain_two, gate_weight, up_weight, down_weight, segment, position, key_mask):
    normed = low(rms(x_rows, gain_one))
    cosine, sine = rope_tables(position.reshape(-1))
    heads_all = query_weight.shape[1] // HD

    def project(weight):
        return low_back(matmul(normed, weight)).reshape(-1, heads_all, HD)
    queries = low(rotate(project(query_weight), cosine, sine))
    keys_all = low(rotate(project(key_weight), cosine, sine))
    mixed = low(mix_weight * project(value_weight) + mix_weight * first_rows.reshape(-1, heads_all, HD))

    def split_groups(tensor):
        return tensor.reshape(N_DP, GROUP, heads_all, HD)
    attended = lax.map(jax.checkpoint(attend_group), (split_groups(queries), split_groups(keys_all), split_groups(mixed), segment, key_mask.reshape(N_DP, GROUP)))
    attended = low(low_back(attended.reshape(-1, heads_all * HD)))
    hidden_rows = x_rows + low_back(matmul(attended, out_weight))
    normed_two = low(rms(hidden_rows, gain_two))
    gate = low_back(matmul(normed_two, gate_weight))
    up_part = low_back(matmul(normed_two, up_weight))
    activation = low(jax.nn.silu(gate) * up_part)
    return hidden_rows + low_back(matmul(activation, down_weight))

def reference(block_input, first_values, lengths, key_mask, attn_gain, query_weight, key_weight, value_weight, out_weight, mixer_gain, gate_weight, up_weight, down_weight, cotangent):
    segment, position = layout(lengths, GROUP)

    def wrapped(x_rows, first_rows, gain_one, weight_q, weight_k, weight_v, weight_o, gain_two, weight_g, weight_u, weight_d):
        return forward(x_rows, first_rows, gain_one, weight_q, weight_k, weight_v, weight_o, gain_two, weight_g, weight_u, weight_d, segment, position, key_mask)
    params = (block_input, first_values.astype(jnp.float32), attn_gain, query_weight.astype(jnp.float32), key_weight.astype(jnp.float32), value_weight.astype(jnp.float32), out_weight.astype(jnp.float32), mixer_gain, gate_weight.astype(jnp.float32), up_weight.astype(jnp.float32), down_weight.astype(jnp.float32))
    output, pullback = jax.vjp(wrapped, *params)
    grads = pullback(cotangent)
    return (output, grads[0], grads[1], grads[3], grads[4], grads[5], grads[6], grads[2], grads[7], grads[8], grads[9], grads[10])
```

```python
import functools

import jax
import jax.numpy as jnp
from jax import lax
from jax.experimental import pallas as pl
from jax.experimental.pallas import tpu as pltpu
from jax.sharding import Mesh, PartitionSpec as P

HD = 64
HALF = 32
EXT = 128
TAIL = 16

epsilon = 1e-05
masked_score = -1e30
mix_weight = 0.5
scale = HD**-0.5

f32 = jnp.float32
bf16 = jnp.bfloat16


def mm(left, right):
    return lax.dot_general(left, right, (((1,), (0,)), ((), ())), preferred_element_type=f32)


def mm_nt(left, right):
    return lax.dot_general(left, right, (((1,), (1,)), ((), ())), preferred_element_type=f32)


def mm_tn(left, right):
    return lax.dot_general(left, right, (((0,), (0,)), ((), ())), preferred_element_type=f32)


def layout(lengths, group_rows):
    ends = jnp.cumsum(lengths, axis=-1)
    starts = ends - lengths
    index = jnp.arange(group_rows, dtype=jnp.int32)
    segment = jnp.sum((index[:, None] >= ends[None, :-1]).astype(jnp.int32), axis=-1)
    number = jnp.arange(lengths.shape[-1], dtype=jnp.int32)
    mine = segment[:, None] == number
    start_of = jnp.sum(jnp.where(mine, starts[None, :], 0), axis=-1)
    end_of = jnp.sum(jnp.where(mine, ends[None, :], 0), axis=-1)
    return segment, index - start_of, start_of, end_of


def rope_tables(position):
    freqs = 10000.0 ** (-2.0 * jnp.arange(HALF, dtype=f32) / HD)
    angles = freqs[:, None] * position.astype(f32)[None, :]
    return jnp.cos(angles), jnp.sin(angles)


def rms_forward(values):
    scale_row = lax.rsqrt(jnp.mean(values * values, axis=-1, keepdims=True) + epsilon)
    return values * scale_row, scale_row


def rms_backward(grad_out, normal, scale_row, gain):
    inner = grad_out * gain
    grad_in = scale_row * (inner - normal * jnp.mean(inner * normal, axis=-1, keepdims=True))
    return grad_in, jnp.sum(grad_out * normal, axis=0)


def row_parts(row):
    high = row.astype(bf16)
    rest = row - high.astype(f32)
    middle = rest.astype(bf16)
    return high.astype(f32), middle.astype(f32), (rest - middle.astype(f32))


def project_kernel(w_ref, g_ref, cos_ref, sin_ref, first_ref, qext_ref, kext_ref, vtail_ref,
                   vext_ref, qx_ref, kx_ref, kt_ref, vt_ref, vx_ref, diag_ref):
    out = mm_nt(w_ref[...], g_ref[...])
    cosine, sine = cos_ref[...], sin_ref[...]

    def rotate(first, second):
        return jnp.concatenate(
            [first * cosine - second * sine, second * cosine + first * sine], axis=0
        ).astype(bf16).astype(f32)

    queries = rotate(out[:HALF], out[HALF:HD]) * scale
    keys = rotate(out[HD : HD + HALF], out[HD + HALF : 2 * HD])
    mixed = (mix_weight * out[2 * HD :] + mix_weight * first_ref[...].astype(f32)).astype(bf16)
    qx_ref[...] = jnp.concatenate([queries.astype(bf16), qext_ref[...]], axis=0)
    kt_ref[...] = keys.astype(bf16)
    kx_ref[...] = jnp.concatenate([keys, kext_ref[...].astype(f32)], axis=0).T.astype(bf16)
    vt_ref[...] = jnp.concatenate([mixed, vtail_ref[...]], axis=0)
    vx_ref[...] = jnp.concatenate([mixed.astype(f32), vext_ref[...].astype(f32)], axis=0).T.astype(bf16)
    diag_ref[...] = jnp.sum(queries * keys, axis=0, keepdims=True)


def project(weights, gathered, cosine, sine, first, qext, kext, vtail, vext, block):
    rows, width = gathered.shape
    steps = rows // block
    column = lambda height: pl.BlockSpec((height, block), lambda i: (0, i))
    fixed = lambda shape: pl.BlockSpec(shape, lambda i: (0, 0))
    return pl.pallas_call(
        project_kernel,
        grid=(steps,),
        in_specs=[
            fixed((3 * HD, width)),
            pl.BlockSpec((block, width), lambda i: (i, 0)),
            column(HALF),
            column(HALF),
            column(HD),
            column(EXT - HD),
            column(EXT - HD),
            column(TAIL),
            fixed((EXT - HD, block)),
        ],
        out_specs=[
            column(EXT),
            pl.BlockSpec((block, EXT), lambda i: (i, 0)),
            column(HD),
            column(HD + TAIL),
            pl.BlockSpec((block, EXT), lambda i: (i, 0)),
            column(1),
        ],
        out_shape=[
            jax.ShapeDtypeStruct((EXT, rows), bf16),
            jax.ShapeDtypeStruct((rows, EXT), bf16),
            jax.ShapeDtypeStruct((HD, rows), bf16),
            jax.ShapeDtypeStruct((HD + TAIL, rows), bf16),
            jax.ShapeDtypeStruct((rows, EXT), bf16),
            jax.ShapeDtypeStruct((1, rows), f32),
        ],
        name="project",
    )(weights, gathered, cosine, sine, first, qext, kext, vtail, vext)


def forward_kernel(low_ref, qx_ref, kx_ref, vt_ref, diag_ref, out_ref, tail_ref, lse_ref):
    step = pl.program_id(0)
    block = qx_ref.shape[1]
    queries = qx_ref[...]

    def update(scores, j, carry):
        top, total = carry
        new_top = jnp.maximum(top, jnp.max(scores, axis=0, keepdims=True))
        weights = jnp.exp(scores - new_top).astype(bf16)
        added = mm(vt_ref[:, pl.ds(pl.multiple_of(j * block, block), block)], weights)
        return new_top, total * jnp.exp(top - new_top) + added

    def score(j):
        return mm(kx_ref[pl.ds(pl.multiple_of(j * block, block), block), :], queries)

    def body(j, carry):
        return update(score(j), j, carry)

    start = (jnp.full((1, block), masked_score, f32), jnp.zeros((HD + TAIL, block), f32))
    carry = lax.fori_loop(low_ref[step], step, body, start)
    down = lax.broadcasted_iota(jnp.int32, (block, block), 0)
    across = lax.broadcasted_iota(jnp.int32, (block, block), 1)
    scores = jnp.where(down < across, score(step), masked_score)
    scores = jnp.where(down == across, diag_ref[...], scores)
    top, total = update(scores, step, carry)
    mass = total[HD : HD + 1]
    out_ref[...] = total[:HD] * (1.0 / mass)
    lse = top + jnp.log(mass)
    lse_ref[...] = lse
    high, middle, low = row_parts(-lse)
    row = lax.broadcasted_iota(jnp.int32, (TAIL, block), 0)
    tail = qx_ref[HD : HD + TAIL, :].astype(f32)
    tail = jnp.where(row == 5, high, jnp.where(row == 6, middle, jnp.where(row == 7, low, tail)))
    tail_ref[...] = tail.astype(bf16)


def attention_forward(lows, qx, kx, vt, diag, block):
    rows = kx.shape[0]
    column = lambda height: pl.BlockSpec((height, block), lambda i, low: (0, i))
    fixed = lambda shape: pl.BlockSpec(shape, lambda i, low: (0, 0))
    return pl.pallas_call(
        forward_kernel,
        grid_spec=pltpu.PrefetchScalarGridSpec(
            num_scalar_prefetch=1,
            grid=(rows // block,),
            in_specs=[column(EXT), fixed(kx.shape), fixed(vt.shape), column(1)],
            out_specs=[column(HD), column(TAIL), column(1)],
        ),
        out_shape=[
            jax.ShapeDtypeStruct((HD, rows), f32),
            jax.ShapeDtypeStruct((TAIL, rows), bf16),
            jax.ShapeDtypeStruct((1, rows), f32),
        ],
        name="attention_forward",
    )(lows, qx, kx, vt, diag)


def backward_kernel(high_ref, qx_ref, tail_ref, kx_ref, kt_ref, vx_ref, diag_ref, lse_ref, out_ref,
                    grad_ref, cos_ref, sin_ref, proj_ref, flat_ref, first_ref,
                    q_all, g_all, dq_all, dk_all, dv_all):
    step = pl.program_id(0)
    steps = pl.num_programs(0)
    block = kx_ref.shape[0]
    rows = qx_ref.shape[1]

    def columns(i):
        return pl.ds(pl.multiple_of(i * block, block), block)

    @pl.when(step == 0)
    def _():
        row = lax.broadcasted_iota(jnp.int32, (TAIL, block), 0)
        zeros = jnp.zeros((EXT - HD - TAIL, block), bf16)

        def prepare(i, carry):
            at = columns(i)
            grads = grad_ref[:, at]
            delta = jnp.sum(grads.astype(f32) * out_ref[:, at], axis=0, keepdims=True)
            high, middle, low = row_parts(-delta)
            tail = jnp.where(row == 0, high, jnp.where(row == 1, middle, jnp.where(row == 2, low, 0.0)))
            g_all[:, at] = jnp.concatenate([grads, tail.astype(bf16), zeros], axis=0)
            q_all[:, at] = jnp.concatenate([qx_ref[:HD, at], tail_ref[:, at], zeros], axis=0)
            dq_all[:, at] = jnp.zeros((HD, block), f32)
            return carry

        lax.fori_loop(0, steps, prepare, 0)

    keys, values, keys_t = kx_ref[...], vx_ref[...], kt_ref[...]

    def visit(i, carry, diagonal):
        dk, dv = carry
        at = columns(i)
        queries, grads = q_all[:, at], g_all[:, at]
        scores = mm(keys, queries)
        if diagonal:
            down = lax.broadcasted_iota(jnp.int32, (block, block), 0)
            across = lax.broadcasted_iota(jnp.int32, (block, block), 1)
            scores = jnp.where(down < across, scores, masked_score)
            scores = jnp.where(down == across, diag_ref[...] - lse_ref[...], scores)
        weights = jnp.exp(scores)
        grad_scores = (weights * mm(values, grads)).astype(bf16)
        dv = dv + mm_nt(weights.astype(bf16), grads[:HD])
        dk = dk + mm_nt(grad_scores, queries[:HD])
        dq_all[:, at] += mm(keys_t, grad_scores)
        return dk, dv

    zero = jnp.zeros((block, HD), f32)
    carry = visit(step, (zero, zero), True)
    dk, dv = lax.fori_loop(step + 1, high_ref[step], lambda i, c: visit(i, c, False), carry)
    dv = dv * mix_weight
    first_ref[...] = dv
    here = columns(step)
    dk_all[:, here] = dk.T
    dv_all[:, here] = dv.T

    @pl.when(step == steps - 1)
    def _():
        width = proj_ref.shape[2]

        def finish(i, carry):
            at = pl.ds(pl.multiple_of(i * width, width), width)
            cosine, sine = cos_ref[:, at], sin_ref[:, at]

            def unrotate(first, second):
                return [first * cosine + second * sine, second * cosine - first * sine]

            dq = dq_all[:, at] * scale
            dk = dk_all[:, at]
            parts = unrotate(dq[:HALF], dq[HALF:]) + unrotate(dk[:HALF], dk[HALF:]) + [dv_all[:, at]]
            result = jnp.concatenate(parts, axis=0).astype(bf16)
            proj_ref[i] = result
            flat_ref[:, at] = result
            return carry

        lax.fori_loop(0, proj_ref.shape[0], finish, 0)


def attention_backward(highs, qx, tail, kx, kt, vx, diag, lse, out, grads, cosine, sine, shards, block):
    rows = kx.shape[0]
    width = rows // shards
    fixed = lambda shape: pl.BlockSpec(shape, lambda i, high: (0,) * len(shape))
    column = lambda height: pl.BlockSpec((height, block), lambda i, high: (0, i))
    row = pl.BlockSpec((block, EXT), lambda i, high: (i, 0))
    return pl.pallas_call(
        backward_kernel,
        grid_spec=pltpu.PrefetchScalarGridSpec(
            num_scalar_prefetch=1,
            grid=(rows // block,),
            in_specs=[
                fixed(qx.shape),
                fixed(tail.shape),
                row,
                column(HD),
                row,
                column(1),
                column(1),
                fixed(out.shape),
                fixed(grads.shape),
                fixed(cosine.shape),
                fixed(sine.shape),
            ],
            out_specs=[
                fixed((shards, 3 * HD, width)),
                fixed((3 * HD, rows)),
                pl.BlockSpec((block, HD), lambda i, high: (i, 0)),
            ],
            scratch_shapes=[
                pltpu.VMEM((EXT, rows), bf16),
                pltpu.VMEM((EXT, rows), bf16),
                pltpu.VMEM((HD, rows), f32),
                pltpu.VMEM((HD, rows), f32),
                pltpu.VMEM((HD, rows), f32),
            ],
        ),
        out_shape=[
            jax.ShapeDtypeStruct((shards, 3 * HD, width), bf16),
            jax.ShapeDtypeStruct((3 * HD, rows), bf16),
            jax.ShapeDtypeStruct((rows, HD), f32),
        ],
        name="attention_backward",
    )(highs, qx, tail, kx, kt, vx, diag, lse, out, grads, cosine, sine)


def extension_rows(segment, key_mask, count):
    rows = segment.shape[0]
    ones = jnp.ones((1, rows), f32)
    number = jnp.arange(count, dtype=jnp.int32)[:, None]
    own = segment[None, :] == number
    bias = jnp.where(key_mask[None, :] == 1, 0.0, masked_score)
    spare = jnp.zeros((EXT - HD - 8, rows), f32)
    qext = jnp.concatenate([ones, own.astype(f32), 0 * ones, 0 * ones, 0 * ones, spare], axis=0)
    kext = jnp.concatenate([bias, jnp.where(own, 0.0, masked_score), ones, ones, ones, spare], axis=0)
    return qext.astype(bf16), kext.astype(bf16)


def block_bounds(start_of, end_of, block):
    lows = start_of[::block] // block
    highs = (end_of[block - 1 :: block] + block - 1) // block
    return lows.astype(jnp.int32), highs.astype(jnp.int32)


def local(
    block_input,
    first_values,
    lengths,
    key_mask,
    attn_gain,
    query_weight,
    key_weight,
    value_weight,
    out_weight,
    mixer_gain,
    gate_weight,
    up_weight,
    down_weight,
    cotangent,
):
    group = ("head", "pair", "side")
    group_rows = first_values.shape[0]
    own_rows, width = block_input.shape
    shards = group_rows // own_rows
    ff_cols = gate_weight.shape[1]
    block = 512
    swap = [(0, 1), (1, 0)]

    normal_one, scale_one = rms_forward(block_input)
    normed_one = (normal_one * attn_gain).astype(bf16)
    gathered_one = lax.all_gather(normed_one, group, axis=0, tiled=True)

    segment, position, start_of, end_of = layout(lengths[0], group_rows)
    cosine, sine = rope_tables(position)
    lows, highs = block_bounds(start_of, end_of, block)
    qext, kext = extension_rows(segment, key_mask, lengths.shape[1])
    row = jnp.arange(EXT - HD, dtype=jnp.int32)[:, None]
    vtail = jnp.broadcast_to((row[:TAIL] == 0).astype(bf16), (TAIL, group_rows))
    vext = jnp.broadcast_to((row < 3).astype(bf16), (EXT - HD, block))
    joined_t = jnp.concatenate([query_weight.T, key_weight.T, value_weight.T], axis=0)
    joined_gate = jnp.concatenate([gate_weight, up_weight], axis=1)

    gathered_one, own_out, own_joined = lax.optimization_barrier((gathered_one, out_weight, joined_t))
    all_out = lax.all_gather(own_out, group, axis=0, tiled=True)
    all_joined = lax.all_gather(own_joined, group, axis=0, tiled=True)

    qx, kx, kt, vt, vx, diag = project(
        joined_t, gathered_one, cosine, sine, first_values.T, qext, kext, vtail, vext, block
    )
    out_t, tail, lse = attention_forward(lows, qx, kx, vt, diag, block)
    sent = out_t.astype(bf16).reshape(HD, shards, own_rows).transpose(1, 0, 2)
    attended_t = lax.all_to_all(sent, group, 0, 0, tiled=True).reshape(shards * HD, own_rows)
    hidden_rows = block_input + mm_tn(attended_t, all_out)

    normal_two, scale_two = rms_forward(hidden_rows)
    normed_two = (normal_two * mixer_gain).astype(bf16)
    grad_low = cotangent.astype(bf16)

    def spread(own):
        other = lax.ppermute(own, "pair", swap)
        both = jnp.concatenate([own, other], axis=0)
        return jnp.concatenate([both, lax.ppermute(both, "side", swap)], axis=0)

    def collect(parts):
        half = parts.shape[0] // 2
        both = parts[:half] + lax.ppermute(parts[half:], "side", swap)
        return both[: half // 2] + lax.ppermute(both[half // 2 :].astype(bf16), "pair", swap).astype(f32)

    gathered_two = spread(normed_two)
    grad_rows = spread(grad_low)
    gate_up = mm(gathered_two, joined_gate)
    gate, up_part = gate_up[:, :ff_cols], gate_up[:, ff_cols:]
    sigma = jax.nn.sigmoid(gate)
    activation = (gate * sigma * up_part).astype(bf16)
    grad_act = mm_nt(grad_rows, down_weight)
    grad_gate = grad_act * up_part * sigma * (1.0 + gate * (1.0 - sigma))
    grad_up = grad_act * gate * sigma
    grad_gate_up = jnp.concatenate([grad_gate, grad_up], axis=1).astype(bf16)
    grad_normed_two = collect(mm_nt(grad_gate_up, joined_gate))
    block_output = hidden_rows + collect(mm(activation, down_weight))
    down_grad = mm_tn(activation, grad_rows)
    gate_up_grad = mm_tn(gathered_two, grad_gate_up)

    grad_norm_two, mixer_gain_part = rms_backward(grad_normed_two, normal_two, scale_two, mixer_gain)
    grad_hidden = cotangent + grad_norm_two
    grad_branch = grad_hidden.astype(bf16)
    out_part = mm(attended_t, grad_branch).astype(bf16)
    out_grad = lax.psum_scatter(out_part, group, scatter_dimension=0, tiled=True)
    sent = mm_nt(all_out, grad_branch).astype(bf16).reshape(shards, HD, own_rows)
    grad_attended = lax.all_to_all(sent, group, 0, 0, tiled=True)
    grad_attended = grad_attended.transpose(1, 0, 2).reshape(HD, group_rows)

    proj_sent, proj_flat, first_grad = attention_backward(
        highs, qx, tail, kx, kt, vx, diag, lse, out_t, grad_attended, cosine, sine, shards, block
    )
    proj_own = lax.all_to_all(proj_sent, group, 0, 0, tiled=True).reshape(shards * 3 * HD, own_rows)
    grad_normed_one = mm_tn(proj_own, all_joined)
    grad_norm_one, attn_gain_part = rms_backward(grad_normed_one, normal_one, scale_one, attn_gain)
    input_grad = grad_hidden + grad_norm_one

    qkv_grad = mm(proj_flat, gathered_one).astype(bf16)
    qkv_grad, out_grad = (
        lax.psum(qkv_grad, "dp").astype(f32),
        lax.psum(out_grad, "dp").astype(f32),
    )
    gate_up_grad, down_grad = lax.psum(
        (gate_up_grad.astype(bf16), down_grad.astype(bf16)), ("dp", "head")
    )
    gate_up_grad, down_grad = gate_up_grad.astype(f32), down_grad.astype(f32)
    attn_gain_grad, mixer_gain_grad = lax.psum((attn_gain_part, mixer_gain_part), ("dp",) + group)
    return (
        block_output,
        input_grad,
        first_grad,
        qkv_grad[:HD].T,
        qkv_grad[HD : 2 * HD].T,
        qkv_grad[2 * HD :].T,
        out_grad,
        attn_gain_grad,
        mixer_gain_grad,
        gate_up_grad[:, :ff_cols],
        gate_up_grad[:, ff_cols:],
        down_grad,
    )


def solution(mesh):
    dp, head, mlp = (mesh.shape[name] for name in ("dp", "head", "mlp"))
    fine = Mesh(mesh.devices.reshape(dp, head, mlp // 2, 2), ("dp", "head", "pair", "side"))
    tokens = P(("dp", "head", "pair", "side"), None)
    head_cols = P(None, ("head", "pair", "side"))
    head_rows = P(("head", "pair", "side"), None)
    ff_cols = P(None, ("pair", "side"))
    ff_rows = P(("pair", "side"), None)
    values = P("dp", ("head", "pair", "side"))
    return jax.shard_map(
        local,
        mesh=fine,
        in_specs=(
            tokens,
            values,
            P("dp", None),
            P("dp"),
            P(),
            head_cols,
            head_cols,
            head_cols,
            head_rows,
            P(),
            ff_cols,
            ff_cols,
            ff_rows,
            tokens,
        ),
        out_specs=(
            tokens,
            tokens,
            values,
            head_cols,
            head_cols,
            head_cols,
            head_rows,
            P(),
            P(),
            ff_cols,
            ff_cols,
            ff_rows,
        ),
        check_vma=False,
    )
```

```python
import functools

import jax
import jax.numpy as jnp
from jax import lax
from jax.experimental import pallas as pl
from jax.experimental.pallas import tpu as pltpu
from jax.sharding import Mesh, PartitionSpec as P

HD = 64
HALF = 32
EXT = 128
TAIL = 16

epsilon = 1e-05
masked_score = -1e30
mix_weight = 0.5
scale = HD**-0.5

f32 = jnp.float32
bf16 = jnp.bfloat16


def mm(left, right):
    return lax.dot_general(left, right, (((1,), (0,)), ((), ())), preferred_element_type=f32)


def mm_nt(left, right):
    return lax.dot_general(left, right, (((1,), (1,)), ((), ())), preferred_element_type=f32)


def mm_tn(left, right):
    return lax.dot_general(left, right, (((0,), (0,)), ((), ())), preferred_element_type=f32)


def layout(lengths, group_rows):
    ends = jnp.cumsum(lengths, axis=-1)
    starts = ends - lengths
    index = jnp.arange(group_rows, dtype=jnp.int32)
    segment = jnp.sum((index[:, None] >= ends[None, :-1]).astype(jnp.int32), axis=-1)
    number = jnp.arange(lengths.shape[-1], dtype=jnp.int32)
    mine = segment[:, None] == number
    start_of = jnp.sum(jnp.where(mine, starts[None, :], 0), axis=-1)
    end_of = jnp.sum(jnp.where(mine, ends[None, :], 0), axis=-1)
    return segment, index - start_of, start_of, end_of


def rope_tables(position):
    freqs = 10000.0 ** (-2.0 * jnp.arange(HALF, dtype=f32) / HD)
    angles = freqs[:, None] * position.astype(f32)[None, :]
    return jnp.cos(angles), jnp.sin(angles)


def rms_forward(values):
    scale_row = lax.rsqrt(jnp.mean(values * values, axis=-1, keepdims=True) + epsilon)
    return values * scale_row, scale_row


def rms_backward(grad_out, normal, scale_row, gain):
    inner = grad_out * gain
    grad_in = scale_row * (inner - normal * jnp.mean(inner * normal, axis=-1, keepdims=True))
    return grad_in, jnp.sum(grad_out * normal, axis=0)


def row_parts(row):
    high = row.astype(bf16)
    rest = row - high.astype(f32)
    middle = rest.astype(bf16)
    return high.astype(f32), middle.astype(f32), (rest - middle.astype(f32))


def project_kernel(w_ref, g_ref, cos_ref, sin_ref, first_ref, qext_ref, kext_ref, vtail_ref,
                   vext_ref, qx_ref, kx_ref, kt_ref, vt_ref, vx_ref, diag_ref):
    out = mm_nt(w_ref[...], g_ref[...])
    cosine, sine = cos_ref[...], sin_ref[...]

    def rotate(first, second):
        return jnp.concatenate(
            [first * cosine - second * sine, second * cosine + first * sine], axis=0
        ).astype(bf16).astype(f32)

    queries = rotate(out[:HALF], out[HALF:HD]) * scale
    keys = rotate(out[HD : HD + HALF], out[HD + HALF : 2 * HD])
    mixed = (mix_weight * out[2 * HD :] + mix_weight * first_ref[...].astype(f32)).astype(bf16)
    qx_ref[...] = jnp.concatenate([queries.astype(bf16), qext_ref[...]], axis=0)
    kt_ref[...] = keys.astype(bf16)
    kx_ref[...] = jnp.concatenate([keys, kext_ref[...].astype(f32)], axis=0).T.astype(bf16)
    vt_ref[...] = jnp.concatenate([mixed, vtail_ref[...]], axis=0)
    vx_ref[...] = jnp.concatenate([mixed.astype(f32), vext_ref[...].astype(f32)], axis=0).T.astype(bf16)
    diag_ref[...] = jnp.sum(queries * keys, axis=0, keepdims=True)


def project(weights, gathered, cosine, sine, first, qext, kext, vtail, vext, block):
    rows, width = gathered.shape
    steps = rows // block
    column = lambda height: pl.BlockSpec((height, block), lambda i: (0, i))
    fixed = lambda shape: pl.BlockSpec(shape, lambda i: (0, 0))
    return pl.pallas_call(
        project_kernel,
        grid=(steps,),
        in_specs=[
            fixed((3 * HD, width)),
            pl.BlockSpec((block, width), lambda i: (i, 0)),
            column(HALF),
            column(HALF),
            column(HD),
            column(EXT - HD),
            column(EXT - HD),
            column(TAIL),
            fixed((EXT - HD, block)),
        ],
        out_specs=[
            column(EXT),
            pl.BlockSpec((block, EXT), lambda i: (i, 0)),
            column(HD),
            column(HD + TAIL),
            pl.BlockSpec((block, EXT), lambda i: (i, 0)),
            column(1),
        ],
        out_shape=[
            jax.ShapeDtypeStruct((EXT, rows), bf16),
            jax.ShapeDtypeStruct((rows, EXT), bf16),
            jax.ShapeDtypeStruct((HD, rows), bf16),
            jax.ShapeDtypeStruct((HD + TAIL, rows), bf16),
            jax.ShapeDtypeStruct((rows, EXT), bf16),
            jax.ShapeDtypeStruct((1, rows), f32),
        ],
        name="project",
        cost_estimate=pl.CostEstimate(flops=8 * HD * rows * width, bytes_accessed=4 * rows * width, transcendentals=0),
    )(weights, gathered, cosine, sine, first, qext, kext, vtail, vext)


def forward_kernel(low_ref, qx_ref, kx_ref, vt_ref, diag_ref, out_ref, tail_ref, lse_ref):
    step = pl.program_id(0)
    block = qx_ref.shape[1]
    queries = qx_ref[...]

    def update(scores, j, carry):
        top, total = carry
        new_top = jnp.maximum(top, jnp.max(scores, axis=0, keepdims=True))
        weights = jnp.exp(scores - new_top).astype(bf16)
        added = mm(vt_ref[:, pl.ds(pl.multiple_of(j * block, block), block)], weights)
        return new_top, total * jnp.exp(top - new_top) + added

    def score(j):
        return mm(kx_ref[pl.ds(pl.multiple_of(j * block, block), block), :], queries)

    def body(j, carry):
        return update(score(j), j, carry)

    start = (jnp.full((1, block), masked_score, f32), jnp.zeros((HD + TAIL, block), f32))
    carry = lax.fori_loop(low_ref[step], step, body, start)
    down = lax.broadcasted_iota(jnp.int32, (block, block), 0)
    across = lax.broadcasted_iota(jnp.int32, (block, block), 1)
    scores = jnp.where(down < across, score(step), masked_score)
    scores = jnp.where(down == across, diag_ref[...], scores)
    top, total = update(scores, step, carry)
    mass = total[HD : HD + 1]
    out_ref[...] = total[:HD] * (1.0 / mass)
    lse = top + jnp.log(mass)
    lse_ref[...] = lse
    high, middle, low = row_parts(-lse)
    row = lax.broadcasted_iota(jnp.int32, (TAIL, block), 0)
    tail = qx_ref[HD : HD + TAIL, :].astype(f32)
    tail = jnp.where(row == 5, high, jnp.where(row == 6, middle, jnp.where(row == 7, low, tail)))
    tail_ref[...] = tail.astype(bf16)


def attention_forward(lows, qx, kx, vt, diag, block):
    rows = kx.shape[0]
    column = lambda height: pl.BlockSpec((height, block), lambda i, low: (0, i))
    fixed = lambda shape: pl.BlockSpec(shape, lambda i, low: (0, 0))
    return pl.pallas_call(
        forward_kernel,
        grid_spec=pltpu.PrefetchScalarGridSpec(
            num_scalar_prefetch=1,
            grid=(rows // block,),
            in_specs=[column(EXT), fixed(kx.shape), fixed(vt.shape), column(1)],
            out_specs=[column(HD), column(TAIL), column(1)],
        ),
        out_shape=[
            jax.ShapeDtypeStruct((HD, rows), f32),
            jax.ShapeDtypeStruct((TAIL, rows), bf16),
            jax.ShapeDtypeStruct((1, rows), f32),
        ],
        name="attention_forward",
        cost_estimate=pl.CostEstimate(flops=HD * rows * rows * 8, bytes_accessed=16 * HD * rows, transcendentals=0),
    )(lows, qx, kx, vt, diag)


def backward_kernel(high_ref, qx_ref, tail_ref, kx_ref, kt_ref, vx_ref, diag_ref, lse_ref, out_ref,
                    grad_ref, cos_ref, sin_ref, proj_ref, flat_ref, first_ref,
                    q_all, g_all, dq_all, dk_all, dv_all):
    step = pl.program_id(0)
    steps = pl.num_programs(0)
    block = kx_ref.shape[0]
    rows = qx_ref.shape[1]

    def columns(i):
        return pl.ds(pl.multiple_of(i * block, block), block)

    @pl.when(step == 0)
    def _():
        row = lax.broadcasted_iota(jnp.int32, (TAIL, block), 0)
        zeros = jnp.zeros((EXT - HD - TAIL, block), bf16)

        def prepare(i, carry):
            at = columns(i)
            grads = grad_ref[:, at]
            delta = jnp.sum(grads.astype(f32) * out_ref[:, at], axis=0, keepdims=True)
            high, middle, low = row_parts(-delta)
            tail = jnp.where(row == 0, high, jnp.where(row == 1, middle, jnp.where(row == 2, low, 0.0)))
            g_all[:, at] = jnp.concatenate([grads, tail.astype(bf16), zeros], axis=0)
            q_all[:, at] = jnp.concatenate([qx_ref[:HD, at], tail_ref[:, at], zeros], axis=0)
            dq_all[:, at] = jnp.zeros((HD, block), f32)
            return carry

        lax.fori_loop(0, steps, prepare, 0)

    keys, values, keys_t = kx_ref[...], vx_ref[...], kt_ref[...]

    def visit(i, carry, diagonal):
        dk, dv = carry
        at = columns(i)
        queries, grads = q_all[:, at], g_all[:, at]
        scores = mm(keys, queries)
        if diagonal:
            down = lax.broadcasted_iota(jnp.int32, (block, block), 0)
            across = lax.broadcasted_iota(jnp.int32, (block, block), 1)
            scores = jnp.where(down < across, scores, masked_score)
            scores = jnp.where(down == across, diag_ref[...] - lse_ref[...], scores)
        weights = jnp.exp(scores)
        grad_scores = (weights * mm(values, grads)).astype(bf16)
        dv = dv + mm_nt(weights.astype(bf16), grads[:HD])
        dk = dk + mm_nt(grad_scores, queries[:HD])
        dq_all[:, at] += mm(keys_t, grad_scores)
        return dk, dv

    zero = jnp.zeros((block, HD), f32)
    carry = visit(step, (zero, zero), True)
    dk, dv = lax.fori_loop(step + 1, high_ref[step], lambda i, c: visit(i, c, False), carry)
    here = columns(step)
    dk_all[:, here] = dk.T
    dv = (dv * mix_weight).T
    dv_all[:, here] = dv
    first_ref[...] = dv

    @pl.when(step == steps - 1)
    def _():
        width = proj_ref.shape[2]

        def finish(i, carry):
            at = pl.ds(pl.multiple_of(i * width, width), width)
            cosine, sine = cos_ref[:, at], sin_ref[:, at]

            def unrotate(first, second):
                return [first * cosine + second * sine, second * cosine - first * sine]

            dq = dq_all[:, at] * scale
            dk = dk_all[:, at]
            parts = unrotate(dq[:HALF], dq[HALF:]) + unrotate(dk[:HALF], dk[HALF:]) + [dv_all[:, at]]
            result = jnp.concatenate(parts, axis=0).astype(bf16)
            proj_ref[i] = result
            flat_ref[:, at] = result
            return carry

        lax.fori_loop(0, proj_ref.shape[0], finish, 0)


def attention_backward(highs, qx, tail, kx, kt, vx, diag, lse, out, grads, cosine, sine, shards, block):
    rows = kx.shape[0]
    width = rows // shards
    fixed = lambda shape: pl.BlockSpec(shape, lambda i, high: (0,) * len(shape))
    column = lambda height: pl.BlockSpec((height, block), lambda i, high: (0, i))
    row = pl.BlockSpec((block, EXT), lambda i, high: (i, 0))
    return pl.pallas_call(
        backward_kernel,
        grid_spec=pltpu.PrefetchScalarGridSpec(
            num_scalar_prefetch=1,
            grid=(rows // block,),
            in_specs=[
                fixed(qx.shape),
                fixed(tail.shape),
                row,
                column(HD),
                row,
                column(1),
                column(1),
                fixed(out.shape),
                fixed(grads.shape),
                fixed(cosine.shape),
                fixed(sine.shape),
            ],
            out_specs=[
                fixed((shards, 3 * HD, width)),
                fixed((3 * HD, rows)),
                column(HD),
            ],
            scratch_shapes=[
                pltpu.VMEM((EXT, rows), bf16),
                pltpu.VMEM((EXT, rows), bf16),
                pltpu.VMEM((HD, rows), f32),
                pltpu.VMEM((HD, rows), f32),
                pltpu.VMEM((HD, rows), f32),
            ],
        ),
        out_shape=[
            jax.ShapeDtypeStruct((shards, 3 * HD, width), bf16),
            jax.ShapeDtypeStruct((3 * HD, rows), bf16),
            jax.ShapeDtypeStruct((HD, rows), f32),
        ],
        name="attention_backward",
        cost_estimate=pl.CostEstimate(flops=HD * rows * rows * 16, bytes_accessed=32 * HD * rows, transcendentals=0),
    )(highs, qx, tail, kx, kt, vx, diag, lse, out, grads, cosine, sine)


def extension_rows(segment, key_mask, count):
    rows = segment.shape[0]
    ones = jnp.ones((1, rows), f32)
    number = jnp.arange(count, dtype=jnp.int32)[:, None]
    own = segment[None, :] == number
    bias = jnp.where(key_mask[None, :] == 1, 0.0, masked_score)
    spare = jnp.zeros((EXT - HD - 8, rows), f32)
    qext = jnp.concatenate([ones, own.astype(f32), 0 * ones, 0 * ones, 0 * ones, spare], axis=0)
    kext = jnp.concatenate([bias, jnp.where(own, 0.0, masked_score), ones, ones, ones, spare], axis=0)
    return qext.astype(bf16), kext.astype(bf16)


def block_bounds(start_of, end_of, block):
    lows = start_of[::block] // block
    highs = (end_of[block - 1 :: block] + block - 1) // block
    return lows.astype(jnp.int32), highs.astype(jnp.int32)


def doubling_sum(value, axis, kind):
    size = lax.axis_size(axis)
    stride = 1
    while stride < size:
        own = value.astype(kind)
        other = lax.ppermute(own, axis, [(i, i ^ stride) for i in range(size)])
        value = own.astype(f32) + other.astype(f32)
        stride *= 2
    return value


def total_sum(value):
    for axis in ("side", "pair", "dp", "head"):
        value = doubling_sum(value, axis, f32)
    return value


def chip_pair_sum(value):
    width = value.shape[1]
    value = value.reshape(lax.axis_size("head"), 2, 2, HD, width)
    for axis, at in (("side", 2), ("pair", 1)):
        me = lax.axis_index(axis)
        own = lax.dynamic_index_in_dim(value, me, at, keepdims=False)
        other = lax.dynamic_index_in_dim(value, 1 - me, at, keepdims=False)
        value = own + lax.ppermute(other.astype(bf16), axis, [(0, 1), (1, 0)]).astype(f32)
    return value


def head_sum(value):
    heads = lax.axis_size("head")
    me = lax.axis_index("head")
    total = lax.dynamic_index_in_dim(value, me, 0, keepdims=False)
    for k in range(1, heads):
        other = lax.dynamic_index_in_dim(value, jnp.bitwise_xor(me, k), 0, keepdims=False)
        pairs = [(i, i ^ k) for i in range(heads)]
        total = total + lax.ppermute(other.astype(bf16), "head", pairs).astype(f32)
    return doubling_sum(total, "dp", bf16)


def local(
    block_input,
    first_values,
    lengths,
    key_mask,
    attn_gain,
    query_weight,
    key_weight,
    value_weight,
    out_weight,
    mixer_gain,
    gate_weight,
    up_weight,
    down_weight,
    cotangent,
):
    group = ("head", "pair", "side")
    group_rows = first_values.shape[0]
    own_rows, width = block_input.shape
    shards = group_rows // own_rows
    ff_cols = gate_weight.shape[1]
    block = 512
    swap = [(0, 1), (1, 0)]

    normal_one, scale_one = rms_forward(block_input)
    normed_one = (normal_one * attn_gain).astype(bf16)
    gathered_one = lax.all_gather(normed_one, group, axis=0, tiled=True)

    segment, position, start_of, end_of = layout(lengths[0], group_rows)
    cosine, sine = rope_tables(position)
    lows, highs = block_bounds(start_of, end_of, block)
    qext, kext = extension_rows(segment, key_mask, lengths.shape[1])
    row = jnp.arange(EXT - HD, dtype=jnp.int32)[:, None]
    vtail = jnp.broadcast_to((row[:TAIL] == 0).astype(bf16), (TAIL, group_rows))
    vext = jnp.broadcast_to((row < 3).astype(bf16), (EXT - HD, block))
    joined_t = jnp.concatenate([query_weight.T, key_weight.T, value_weight.T], axis=0)
    joined_gate = jnp.concatenate([gate_weight.T, up_weight.T], axis=0)

    grad_low = cotangent.astype(bf16)
    gathered_one, own_out, joined_t, joined_gate, grad_low, cosine, sine, qext, kext, vtail, vext, lows, highs = (
        lax.optimization_barrier(
            (gathered_one, out_weight, joined_t, joined_gate, grad_low, cosine, sine, qext, kext, vtail, vext, lows, highs)
        )
    )
    all_out = lax.all_gather(own_out, group, axis=0, tiled=True)

    def spread(own):
        far = lax.ppermute(own, "pair", swap)
        near = lax.ppermute(own, "side", swap)
        return jnp.concatenate([own, near], axis=0), far

    def spread_far(far):
        return jnp.concatenate([far, lax.ppermute(far, "side", swap)], axis=0)

    def fold(part):
        return part[:own_rows] + lax.ppermute(part[own_rows:], "side", swap)

    def return_far(part):
        return lax.ppermute(part.astype(bf16), "pair", swap).astype(f32)

    qx, kx, kt, vt, vx, diag = project(
        joined_t, gathered_one, cosine, sine, first_values.T, qext, kext, vtail, vext, block
    )
    grad_low, qx = lax.optimization_barrier((grad_low, qx))
    rows_near, rows_far = spread(grad_low)
    out_t, tail, lse = attention_forward(lows, qx, kx, vt, diag, block)
    out_t, rows_near, rows_far, all_out, own_joined = lax.optimization_barrier(
        (out_t, rows_near, rows_far, all_out, joined_t)
    )
    sent = out_t.astype(bf16).reshape(HD, shards, own_rows).transpose(1, 0, 2)
    attended_t = lax.all_to_all(sent, group, 0, 0, tiled=True).reshape(shards * HD, own_rows)
    attended_t, own_joined = lax.optimization_barrier((attended_t, own_joined))
    all_joined = lax.all_gather(own_joined, group, axis=0, tiled=True)
    hidden_rows = block_input + mm_tn(attended_t, all_out)

    normal_two, scale_two = rms_forward(hidden_rows)
    normed_two = (normal_two * mixer_gain).astype(bf16)
    two_near, two_far = spread(normed_two)

    def mixer(rows, grads):
        gate_up = mm_nt(joined_gate, rows)
        gate, up_part = gate_up[:ff_cols], gate_up[ff_cols:]
        sigma = jax.nn.sigmoid(gate)
        activation = (gate * sigma * up_part).astype(bf16)
        grad_act = mm_nt(down_weight, grads)
        grad_gate = grad_act * up_part * sigma * (1.0 + gate * (1.0 - sigma))
        grad_up = grad_act * gate * sigma
        grad_gate_up = jnp.concatenate([grad_gate, grad_up], axis=0).astype(bf16)
        return activation, grad_gate_up, mm_tn(grad_gate_up, joined_gate)

    act_near, grads_near, back_near = mixer(two_near, rows_near)
    gate_up_near = mm(grads_near, two_near)
    down_near = mm(act_near, rows_near)
    two_far, gate_up_near, down_near, back_near = lax.optimization_barrier(
        (two_far, gate_up_near, down_near, back_near)
    )
    back_near = fold(back_near)
    two_far = spread_far(two_far)
    rows_far = spread_far(rows_far)
    act_far, grads_far, back_far = mixer(two_far, rows_far)
    back_far, act_far, grads_far = lax.optimization_barrier(
        (fold(back_far).astype(bf16), act_far, grads_far)
    )
    back_far = return_far(back_far)
    gate_up_grad = (gate_up_near + mm(grads_far, two_far)).astype(bf16)
    down_grad = (down_near + mm(act_far, rows_far)).astype(bf16)
    back_far, _, _ = lax.optimization_barrier((back_far, down_grad, gate_up_grad))
    grad_normed_two = back_near + back_far
    gate_up_grad, down_grad = lax.psum((gate_up_grad, down_grad), ("dp", "head"))

    grad_norm_two, mixer_gain_part = rms_backward(grad_normed_two, normal_two, scale_two, mixer_gain)
    grad_hidden = cotangent + grad_norm_two
    grad_branch = grad_hidden.astype(bf16)
    sent = mm_nt(all_out, grad_branch).astype(bf16).reshape(shards, HD, own_rows)
    sent, act_near, act_far = lax.optimization_barrier((sent, act_near, act_far))
    grad_attended = lax.all_to_all(sent, group, 0, 0, tiled=True)
    down_part = fold(mm_tn(act_near, down_weight)) + return_far(fold(mm_tn(act_far, down_weight)))
    block_output = hidden_rows + down_part
    out_part = chip_pair_sum(mm(attended_t, grad_branch))
    grad_attended = grad_attended.transpose(1, 0, 2).reshape(HD, group_rows)

    proj_sent, proj_flat, first_grad = attention_backward(
        highs, qx, tail, kx, kt, vx, diag, lse, out_t, grad_attended, cosine, sine, shards, block
    )
    proj_own = lax.all_to_all(proj_sent, group, 0, 0, tiled=True).reshape(shards * 3 * HD, own_rows)
    qkv_grad = mm(proj_flat, gathered_one)
    proj_own, out_part, qkv_grad, block_output = lax.optimization_barrier(
        (proj_own, out_part, qkv_grad, block_output)
    )
    grad_normed_one = mm_tn(proj_own, all_joined)
    grad_norm_one, attn_gain_part = rms_backward(grad_normed_one, normal_one, scale_one, attn_gain)
    input_grad = grad_hidden + grad_norm_one
    out_grad = head_sum(out_part)
    qkv_grad = doubling_sum(qkv_grad, "dp", bf16)
    gains = total_sum(jnp.stack([attn_gain_part, mixer_gain_part]))
    attn_gain_grad, mixer_gain_grad = gains[0], gains[1]
    gate_up_grad, down_grad = gate_up_grad.astype(f32), down_grad.astype(f32)
    return (
        block_output,
        input_grad,
        first_grad.T,
        qkv_grad[:HD].T,
        qkv_grad[HD : 2 * HD].T,
        qkv_grad[2 * HD :].T,
        out_grad,
        attn_gain_grad,
        mixer_gain_grad,
        gate_up_grad[:ff_cols].T,
        gate_up_grad[ff_cols:].T,
        down_grad,
    )


def solution(mesh):
    dp, head, mlp = (mesh.shape[name] for name in ("dp", "head", "mlp"))
    fine = Mesh(mesh.devices.reshape(dp, head, mlp // 2, 2), ("dp", "head", "pair", "side"))
    tokens = P(("dp", "head", "pair", "side"), None)
    head_cols = P(None, ("head", "pair", "side"))
    head_rows = P(("head", "pair", "side"), None)
    ff_cols = P(None, ("pair", "side"))
    ff_rows = P(("pair", "side"), None)
    values = P("dp", ("head", "pair", "side"))
    return jax.shard_map(
        local,
        mesh=fine,
        in_specs=(
            tokens,
            values,
            P("dp", None),
            P("dp"),
            P(),
            head_cols,
            head_cols,
            head_cols,
            head_rows,
            P(),
            ff_cols,
            ff_cols,
            ff_rows,
            tokens,
        ),
        out_specs=(
            tokens,
            tokens,
            values,
            head_cols,
            head_cols,
            head_cols,
            head_rows,
            P(),
            P(),
            ff_cols,
            ff_cols,
            ff_rows,
        ),
        check_vma=False,
    )
```
